512 devices in a mesh: row: 16 (over x_hi, y), col: 8 (over z), depth: 4 (over x_lo, core).
Axes of the slice: x: 4 (x_hi: 2, x_lo: 2; x = x_hi * 2 + x_lo), y: 8, z: 8, core: 2. Of those that a mesh axis runs over, the one named last changes fastest.
Arguments:
- x_vals: bfloat16 [16, 64, 4, 128, 128], P('row', ('col', 'depth')), may hold values from -2.5 to 2.5
- x_rows: int32 [16, 64, 4], P('row', ('col', 'depth')), may hold values from -1 to 3, as said below
- out_block: int32 [16, 8, 4], P('row', 'col', 'depth'), may hold values from 0 to 15, as said below
Outputs:
- product_blocks: bfloat16 [16, 8, 4, 128, 128], P('row', 'col', 'depth')
The draws below stay inside these ranges and needn't reach their ends.
Inputs may be any that keep to these rules, and one draw needn't show every extreme that they name: `x_rows`: within one row group and block column the filled slots name distinct rows. In every row group, each run of 2 block columns that starts at a multiple of 2 has a column with all 4 slots filled. `out_block`: within one tile the 4 entries are distinct positions, and every tile lists position 15 among them.
All inputs are finite; a program needn't handle non-finite values.
Results may differ from the reference program's by a relative error of at most 0.001.
Values may be sent and summed in bfloat16 or wider, within the bound.
No kernel may reach another device: no remote copies, remote signals or barrier semaphores. Data moves between devices by JAX's collectives and lax.ppermute only.
A program may use at most 128 MiB of HBM per device.

```python
import jax
import jax.numpy as jnp
from jax import lax

BS = 128
PW = 2
H = 4
NB = 64
RG = 4
OG = 4
N_ROW = 16
N_COL = 8


def draw_x_rows(key, part):
    cell_count = N_ROW * NB
    key_order, key_force, key_count = jax.random.split(key, 3)
    spread = jnp.arange(RG, dtype=jnp.int32)
    scores = jax.random.randint(key_order, (cell_count, RG), 0, 1 << 16, dtype=jnp.int32) * RG + spread[None, :]
    chosen_col = jax.random.randint(key_force, (N_ROW, NB // PW), 0, PW, dtype=jnp.int32)
    column = jnp.arange(NB, dtype=jnp.int32)
    forced = column[None, :] % PW == jnp.repeat(chosen_col, PW, axis=1)
    forced = forced.reshape(cell_count)
    ranking = jnp.argsort(scores, axis=1)[:, :H].astype(jnp.int32)
    counts = jax.random.randint(key_count, (cell_count,), 0, H + 1, dtype=jnp.int32)
    counts = jnp.where(forced, H, counts)
    slot_index = jnp.arange(H, dtype=jnp.int32)
    row_ids = jnp.where(slot_index[None, :] < counts[:, None], ranking, -1)
    return row_ids.reshape(N_ROW, NB, H)


def draw_out_block(key, part):
    tile_count = N_ROW * N_COL
    span_size = RG * RG
    key_pick, key_mix = jax.random.split(key, 2)
    spread = jnp.arange(span_size, dtype=jnp.int32)
    scores = jax.random.randint(key_pick, (tile_count, span_size), 0, 1 << 16, dtype=jnp.int32) * span_size + spread[None, :]
    scores = jnp.where(spread[None, :] == span_size - 1, -1, scores)
    chosen = jnp.argsort(scores, axis=1)[:, :OG].astype(jnp.int32)
    entry_spread = jnp.arange(OG, dtype=jnp.int32)
    mixing = jax.random.randint(key_mix, (tile_count, OG), 0, 1 << 16, dtype=jnp.int32) * OG + entry_spread[None, :]
    mixing = jnp.argsort(mixing, axis=1).astype(jnp.int32)
    chosen = jnp.take_along_axis(chosen, mixing, axis=1)
    return chosen.reshape(N_ROW, N_COL, OG)


def block_levels(key, shape, cuts, least, top_value):
    def one(position, parts):
        heights = jax.random.uniform(jax.random.fold_in(jax.random.fold_in(key, 6), position), (parts,), jnp.float32, least / len(cuts), top_value / len(cuts))
        return jnp.repeat(jnp.exp(heights), shape[position] // parts).reshape((-1,) + (1,) * (len(shape) - position - 1))

    loudness = one(*cuts[0])
    for cut in cuts[1:]:
        loudness = loudness * one(*cut)
    return loudness


def gaussian(own_key, extent, scale, reach, shards=(), kind=jnp.bfloat16):
    gain = block_levels(own_key, extent, shards, -0.22, 0.18) if shards else 1.0
    drawn = jax.random.normal(own_key, extent, jnp.float32) * scale * gain
    return jnp.minimum(jnp.maximum(drawn, -reach), reach).astype(kind)


def setup_inputs(seed: int = 0) -> dict:
    key_of = jax.random.split(jax.random.key(seed), 4)
    return {
        "x_vals": gaussian(key_of[0], (N_ROW, NB, H, BS, BS), 0.18, 2.5, ((0, 16), (1, 32))),
        "x_rows": draw_x_rows(jax.random.fold_in(key_of[3], 71), 0),
        "out_block": draw_out_block(jax.random.fold_in(key_of[3], 71), 0),
    }


def tile_sum(left_vals, left_rows, right_vals, right_rows, positions):
    partial_value = jnp.zeros((positions.shape[0], left_vals.shape[2], left_vals.shape[3]), jnp.float32)
    slot_total = left_vals.shape[0] * left_vals.shape[1]
    left_valid = left_rows >= 0
    left_wide = left_vals.astype(jnp.float32)
    for slot_index in range(right_vals.shape[1]):
        partner_slot = right_vals[:, slot_index].astype(jnp.float32)
        right_slot_rows = right_rows[:, slot_index]
        blocks = jnp.einsum("ksab,kcb->ksac", left_wide, partner_slot, precision=lax.Precision.HIGHEST)
        target = left_rows * RG + right_slot_rows[:, None]
        target = jnp.where(left_valid & (right_slot_rows >= 0)[:, None], target, -1)
        select = (target.reshape(1, slot_total) == positions[:, None]).astype(jnp.float32)
        gained = jnp.dot(select, blocks.reshape(slot_total, -1), precision=lax.Precision.HIGHEST)
        partial_value = partial_value + gained.reshape(partial_value.shape)
    return partial_value


def reference(x_vals, x_rows, out_block):
    listed = out_block.reshape(N_ROW * N_COL, OG)

    def one_tile(tile_index):
        row_group = tile_index // N_COL
        offset = tile_index % N_COL
        partner_group = (row_group + offset - N_COL // 2) % N_ROW
        left_vals = lax.dynamic_index_in_dim(x_vals, row_group, 0, keepdims=False)
        left_rows = lax.dynamic_index_in_dim(x_rows, row_group, 0, keepdims=False)
        right_vals = lax.dynamic_index_in_dim(x_vals, partner_group, 0, keepdims=False)
        right_rows = lax.dynamic_index_in_dim(x_rows, partner_group, 0, keepdims=False)
        positions = lax.dynamic_index_in_dim(listed, tile_index, 0, keepdims=False)
        return tile_sum(left_vals, left_rows, right_vals, right_rows, positions).astype(jnp.bfloat16)

    result = lax.map(one_tile, jnp.arange(N_ROW * N_COL, dtype=jnp.int32))
    return result.reshape(N_ROW, N_COL, OG, BS, BS)
```

```python
import jax
import jax.numpy as jnp
from jax import lax
from jax.experimental import pallas as pl
from jax.experimental.pallas import tpu as pltpu
from jax.sharding import PartitionSpec as P

TILES = ((2, -2), (1, -2), (0, -2), (0, -1), (0, 0), (0, 1), (0, 2), (-1, 2))

LEVELS = 32766.0
TAIL = 8


def dense_kernel(rows_ref, vals_ref, out_ref):
    width = vals_ref.shape[-1]
    for column in range(vals_ref.shape[0]):
        for row in range(out_ref.shape[0]):
            slot = jnp.int32(-1)
            for candidate in range(vals_ref.shape[1]):
                slot = jnp.where(rows_ref[column, candidate] == row, candidate, slot)
            lanes = slice(column * width, (column + 1) * width)

            @pl.when(slot >= 0)
            def _():
                out_ref[row, :, lanes] = vals_ref[column, slot]

            @pl.when(slot < 0)
            def _():
                out_ref[row, :, lanes] = jnp.zeros(vals_ref.shape[2:], out_ref.dtype)


def densify(x_vals, x_rows):
    columns, slots, size, width = x_vals.shape
    return pl.pallas_call(
        dense_kernel,
        out_shape=jax.ShapeDtypeStruct((slots, size, columns * width), x_vals.dtype),
        in_specs=[pl.BlockSpec(memory_space=pltpu.SMEM), pl.BlockSpec(memory_space=pltpu.VMEM)],
        out_specs=pl.BlockSpec(memory_space=pltpu.VMEM),
    )(x_rows, x_vals)


def step_of(exponent, mantissa):
    return mantissa.astype(jnp.float32) * jnp.exp2((exponent - 14).astype(jnp.float32)) * (1.0 / LEVELS)


def encode(value, code_ref):
    size = value.shape[0]
    peak = jnp.maximum(jnp.max(jnp.abs(value), axis=0, keepdims=True), 1e-30)
    exponent = jnp.ceil(jnp.log2(peak))
    mantissa = jnp.ceil(peak * jnp.exp2(14.0 - exponent)) + 1.0
    exponent = exponent.astype(jnp.int32)
    mantissa = mantissa.astype(jnp.int32)
    code = jnp.floor(value * (1.0 / step_of(exponent, mantissa)) + 0.5)
    code_ref[:size] = code.astype(jnp.int32).astype(jnp.int16)
    line = lax.broadcasted_iota(jnp.int32, (TAIL, value.shape[1]), 0)
    tail = jnp.where(line == 0, exponent, jnp.where(line == 1, mantissa, 0))
    code_ref[size:] = tail.astype(jnp.int16)


def decode_sum_kernel(code_ref, out_ref):
    size = out_ref.shape[0]
    total = None
    for part in range(code_ref.shape[0]):
        tail = code_ref[part, size:].astype(jnp.int32)
        value = code_ref[part, :size].astype(jnp.int32).astype(jnp.float32) * step_of(tail[0:1], tail[1:2])
        total = value if total is None else total + value
    out_ref[...] = total.astype(out_ref.dtype)


def decode_sum(codes):
    size = codes.shape[2]
    vmem = pl.BlockSpec(memory_space=pltpu.VMEM)
    return pl.pallas_call(
        decode_sum_kernel,
        out_shape=jax.ShapeDtypeStruct((size, size), jnp.bfloat16),
        in_specs=[vmem],
        out_specs=vmem,
    )(codes)


def gram_kernel(positions_ref, own, own_other, below, above, near_other, below2, above2, far_other, out_ref):
    halves = {
        0: (own, own_other),
        -1: (below, near_other.at[0]),
        1: (above, near_other.at[1]),
        -2: (below2, far_other.at[0]),
        2: (above2, far_other.at[1]),
    }
    for tile, (left, right) in enumerate(TILES):
        for chip in range(out_ref.shape[1]):
            position = positions_ref[tile, chip]
            left_row = lax.shift_right_logical(position, 2)
            right_row = lax.bitwise_and(position, 3)
            total = None
            for left_ref, right_ref in zip(halves[left], halves[right]):
                product = lax.dot_general(
                    left_ref[left_row],
                    right_ref[right_row],
                    (((1,), (1,)), ((), ())),
                    preferred_element_type=jnp.float32,
                )
                total = product if total is None else total + product
            encode(total, out_ref.at[tile, chip])


def gram_blocks(positions, items):
    size = items[0].shape[1]
    vmem = pl.BlockSpec(memory_space=pltpu.VMEM)
    return pl.pallas_call(
        gram_kernel,
        out_shape=jax.ShapeDtypeStruct(positions.shape + (size + TAIL, size), jnp.int16),
        in_specs=[pl.BlockSpec(memory_space=pltpu.SMEM)] + [vmem] * len(items),
        out_specs=vmem,
        compiler_params=pltpu.CompilerParams(vmem_limit_bytes=48 * 2**20),
    )(positions, *items)


def moved(value, axis, target):
    count = lax.axis_size(axis)
    return lax.ppermute(value, axis, [(source, target(source)) for source in range(count)])


def on_device(x_vals, x_rows, out_block):
    row_count = lax.axis_size("row")
    col_count = lax.axis_size("col")
    chip_count = lax.axis_size("chip")

    def up(value):
        return moved(value, "row", lambda r: (r + 1) % row_count)

    def down(value):
        return moved(value, "row", lambda r: (r - 1) % row_count)

    def swap_core(value):
        return moved(value, "core", lambda c: c ^ 1)

    def to_worker(place):
        row, col = divmod(place, col_count)
        return (row - TILES[col][0]) % row_count * col_count + col

    def to_home(place):
        row, col = divmod(place, col_count)
        return (row + TILES[col][0]) % row_count * col_count + col

    wanted = moved(out_block.reshape(1), ("row", "col"), to_worker)
    own = densify(x_vals[0], x_rows[0])
    own, wanted = lax.optimization_barrier((own, wanted))
    below = up(own)
    above = down(own)
    spread = jnp.broadcast_to(wanted.reshape(1, 1), (col_count * chip_count, 128))
    late_own, spread = lax.optimization_barrier((own, spread))
    own_other = swap_core(late_own)
    positions = lax.all_to_all(spread, ("col", "chip"), 0, 0, tiled=True)
    positions = positions[:, 0].reshape(col_count, chip_count)
    below, above, own_other, positions = lax.optimization_barrier((below, above, own_other, positions))
    below2 = up(below)
    above2 = down(above)
    near_other = swap_core(jnp.stack([below, above]))
    far_other = swap_core(jnp.stack([below2, above2]))
    partial_sums = gram_blocks(
        positions, (own, own_other, below, above, near_other, below2, above2, far_other)
    )
    partial_sums = partial_sums.reshape((-1,) + partial_sums.shape[2:])
    gathered = lax.all_to_all(partial_sums, ("col", "chip"), 0, 0, tiled=True)
    total = decode_sum(gathered)
    result = moved(total, ("row", "col"), to_home)
    return result.reshape(out_block.shape + x_vals.shape[3:])


def solution(mesh):
    shape = dict(mesh.shape)
    devices = mesh.devices.reshape(shape["row"], shape["col"], shape["depth"] // 2, 2)
    fine_mesh = jax.sharding.Mesh(devices, ("row", "col", "chip", "core"))
    depth = ("chip", "core")
    in_specs = (
        P("row", ("col",) + depth, None, None, None),
        P("row", ("col",) + depth, None),
        P("row", "col", depth),
    )
    out_specs = P("row", "col", depth, None, None)
    return jax.shard_map(
        on_device, mesh=fine_mesh, in_specs=in_specs, out_specs=out_specs, check_vma=False
    )
```

```python
import jax
import jax.numpy as jnp
from jax import lax
from jax.experimental import pallas as pl
from jax.experimental.pallas import tpu as pltpu
from jax.sharding import PartitionSpec as P

TILES = ((2, -2), (1, -2), (0, -2), (0, -1), (0, 0), (0, 1), (0, 2), (-1, 2))

LEVELS = 32766.0
TAIL = 8
NOTE = 16


def dense_kernel(rows_ref, wanted_ref, vals_ref, out_ref):
    columns, slots, size, width = vals_ref.shape
    for column in range(columns):
        for row in range(slots):
            slot = jnp.int32(-1)
            for candidate in range(slots):
                slot = jnp.where(rows_ref[column, candidate] == row, candidate, slot)
            at = (slice(row * size, (row + 1) * size), slice(column * width, (column + 1) * width))

            @pl.when(slot >= 0)
            def _():
                out_ref[at] = vals_ref[column, slot]

            @pl.when(slot < 0)
            def _():
                out_ref[at] = jnp.zeros((size, width), out_ref.dtype)

    note = jnp.full((NOTE, columns * width), wanted_ref[0], jnp.int32)
    out_ref[slots * size :] = note.astype(jnp.float32).astype(out_ref.dtype)


def densify(x_vals, x_rows, wanted):
    columns, slots, size, width = x_vals.shape
    smem = pl.BlockSpec(memory_space=pltpu.SMEM)
    vmem = pl.BlockSpec(memory_space=pltpu.VMEM)
    return pl.pallas_call(
        dense_kernel,
        out_shape=jax.ShapeDtypeStruct((slots * size + NOTE, columns * width), x_vals.dtype),
        in_specs=[smem, smem, vmem],
        out_specs=vmem,
    )(x_rows, wanted, x_vals)


def step_of(exponent, mantissa):
    return mantissa.astype(jnp.float32) * jnp.exp2((exponent - 14).astype(jnp.float32)) * (1.0 / LEVELS)


def encode(value, code_ref):
    size = value.shape[0]
    peak = jnp.maximum(jnp.max(jnp.abs(value), axis=0, keepdims=True), 1e-30)
    exponent = jnp.ceil(jnp.log2(peak))
    mantissa = jnp.ceil(peak * jnp.exp2(14.0 - exponent)) + 1.0
    exponent = exponent.astype(jnp.int32)
    mantissa = mantissa.astype(jnp.int32)
    code = jnp.floor(value * (1.0 / step_of(exponent, mantissa)) + 0.5)
    code_ref[:size] = code.astype(jnp.int32).astype(jnp.int16)
    line = lax.broadcasted_iota(jnp.int32, (TAIL, value.shape[1]), 0)
    tail = jnp.where(line == 0, exponent, jnp.where(line == 1, mantissa, 0))
    code_ref[size:] = tail.astype(jnp.int16)


def decode_sum_kernel(code_ref, out_ref):
    size = out_ref.shape[0]
    total = None
    for part in range(code_ref.shape[0]):
        tail = code_ref[part, size:].astype(jnp.int32)
        value = code_ref[part, :size].astype(jnp.int32).astype(jnp.float32) * step_of(tail[0:1], tail[1:2])
        total = value if total is None else total + value
    out_ref[...] = total.astype(out_ref.dtype)


def decode_sum(codes):
    size = codes.shape[2]
    vmem = pl.BlockSpec(memory_space=pltpu.VMEM)
    return pl.pallas_call(
        decode_sum_kernel,
        out_shape=jax.ShapeDtypeStruct((size, size), jnp.bfloat16),
        in_specs=[vmem],
        out_specs=vmem,
    )(codes)


def gram_kernel(positions_ref, own, own_other, below, above, near_other, below2, above2, below2_other, above2_other, out_ref):
    halves = {
        0: (own, own_other),
        -1: (below, near_other.at[0]),
        1: (above, near_other.at[1]),
        -2: (below2, below2_other),
        2: (above2, above2_other),
    }
    for tile, (left, right) in enumerate(TILES):
        for chip in range(out_ref.shape[1]):
            position = positions_ref[tile, chip]
            size = out_ref.shape[3]
            left_row = pl.ds(pl.multiple_of(lax.shift_right_logical(position, 2) * size, size), size)
            right_row = pl.ds(pl.multiple_of(lax.bitwise_and(position, 3) * size, size), size)
            total = None
            for left_ref, right_ref in zip(halves[left], halves[right]):
                product = lax.dot_general(
                    left_ref[left_row, :],
                    right_ref[right_row, :],
                    (((1,), (1,)), ((), ())),
                    preferred_element_type=jnp.float32,
                )
                total = product if total is None else total + product
            encode(total, out_ref.at[tile, chip])


def gram_blocks(positions, items, size):
    vmem = pl.BlockSpec(memory_space=pltpu.VMEM)
    return pl.pallas_call(
        gram_kernel,
        out_shape=jax.ShapeDtypeStruct(positions.shape + (size + TAIL, size), jnp.int16),
        in_specs=[pl.BlockSpec(memory_space=pltpu.SMEM)] + [vmem] * len(items),
        out_specs=vmem,
        compiler_params=pltpu.CompilerParams(vmem_limit_bytes=48 * 2**20),
    )(positions, *items)


def moved(value, axis, target):
    count = lax.axis_size(axis)
    return lax.ppermute(value, axis, [(source, target(source)) for source in range(count)])


def on_device(x_vals, x_rows, out_block):
    row_count = lax.axis_size("row")
    col_count = lax.axis_size("col")
    chip_count = lax.axis_size("chip")

    def up(value):
        return moved(value, "row", lambda r: (r + 1) % row_count)

    def down(value):
        return moved(value, "row", lambda r: (r - 1) % row_count)

    def swap_core(value):
        return moved(value, "core", lambda c: c ^ 1)

    def to_home(place):
        row, col = divmod(place, col_count)
        return (row + TILES[col][0]) % row_count * col_count + col

    own = densify(x_vals[0], x_rows[0], out_block.reshape(1))
    below = up(own)
    above = down(own)
    below2 = up(below)
    above2 = down(above)
    late_own, near = lax.optimization_barrier((own, jnp.stack([below, above])))
    near_other = swap_core(near)
    own_other = swap_core(late_own)
    above2_other = swap_core(above2)
    col = lax.axis_index("col")
    wanted = own[-1, :128]
    for shift, item in ((2, above2), (1, above), (-1, below)):
        for tile, (left, _) in enumerate(TILES):
            if left == shift:
                wanted = jnp.where(col == tile, item[-1, :128], wanted)
    spread = jnp.broadcast_to(wanted.astype(jnp.float32), (col_count * chip_count, 128))
    gathered_positions = lax.all_to_all(spread, ("col", "chip"), 0, 0, tiled=True)
    below2, gathered_positions = lax.optimization_barrier((below2, gathered_positions))
    positions = gathered_positions[:, 0].astype(jnp.int32).reshape(col_count, chip_count)
    below2_other = swap_core(below2)
    partial_sums = gram_blocks(
        positions, (own, own_other, below, above, near_other, below2, above2, below2_other, above2_other), x_vals.shape[3]
    )
    partial_sums = partial_sums.reshape((-1,) + partial_sums.shape[2:])
    gathered = lax.all_to_all(partial_sums, ("col", "chip"), 0, 0, tiled=True)
    total = decode_sum(gathered)
    result = moved(total, ("row", "col"), to_home)
    return result.reshape(out_block.shape + x_vals.shape[3:])


def solution(mesh):
    shape = dict(mesh.shape)
    devices = mesh.devices.reshape(shape["row"], shape["col"], shape["depth"] // 2, 2)
    fine_mesh = jax.sharding.Mesh(devices, ("row", "col", "chip", "core"))
    depth = ("chip", "core")
    in_specs = (
        P("row", ("col",) + depth, None, None, None),
        P("row", ("col",) + depth, None),
        P("row", "col", depth),
    )
    out_specs = P("row", "col", depth, None, None)
    return jax.shard_map(
        on_device, mesh=fine_mesh, in_specs=in_specs, out_specs=out_specs, check_vma=False
    )
```

```python
import jax
import jax.numpy as jnp
from jax import lax
from jax.experimental import pallas as pl
from jax.experimental.pallas import tpu as pltpu
from jax.sharding import PartitionSpec as P

TILES = ((2, -2), (1, -2), (0, -2), (0, -1), (0, 0), (0, 1), (0, 2), (-1, 2))

NEAR = (3, 4, 5, 6, 7)
FAR = (0, 1, 2)
LEVELS = 32766.0
TAIL = 8
NOTE = 16


def dense_kernel(rows_ref, wanted_ref, vals_ref, out_ref):
    columns, slots, size, width = vals_ref.shape
    for column in range(columns):
        for row in range(slots):
            slot = jnp.int32(-1)
            for candidate in range(slots):
                slot = jnp.where(rows_ref[column, candidate] == row, candidate, slot)
            at = (slice(row * size, (row + 1) * size), slice(column * width, (column + 1) * width))

            @pl.when(slot >= 0)
            def _():
                out_ref[at] = vals_ref[column, slot]

            @pl.when(slot < 0)
            def _():
                out_ref[at] = jnp.zeros((size, width), out_ref.dtype)

    note = jnp.full((NOTE, columns * width), wanted_ref[0], jnp.int32)
    out_ref[slots * size :] = note.astype(jnp.float32).astype(out_ref.dtype)


def densify(x_vals, x_rows, wanted):
    columns, slots, size, width = x_vals.shape
    smem = pl.BlockSpec(memory_space=pltpu.SMEM)
    vmem = pl.BlockSpec(memory_space=pltpu.VMEM)
    return pl.pallas_call(
        dense_kernel,
        out_shape=jax.ShapeDtypeStruct((slots * size + NOTE, columns * width), x_vals.dtype),
        in_specs=[smem, smem, vmem],
        out_specs=vmem,
    )(x_rows, wanted, x_vals)


def step_of(exponent, mantissa):
    return mantissa.astype(jnp.float32) * jnp.exp2((exponent - 14).astype(jnp.float32)) * (1.0 / LEVELS)


def encode(value, code_ref):
    size = value.shape[0]
    peak = jnp.maximum(jnp.max(jnp.abs(value), axis=0, keepdims=True), 1e-30)
    exponent = jnp.ceil(jnp.log2(peak))
    mantissa = jnp.ceil(peak * jnp.exp2(14.0 - exponent)) + 1.0
    exponent = exponent.astype(jnp.int32)
    mantissa = mantissa.astype(jnp.int32)
    code = jnp.floor(value * (1.0 / step_of(exponent, mantissa)) + 0.5)
    code_ref[:size] = code.astype(jnp.int32).astype(jnp.int16)
    line = lax.broadcasted_iota(jnp.int32, (TAIL, value.shape[1]), 0)
    tail = jnp.where(line == 0, exponent, jnp.where(line == 1, mantissa, 0))
    code_ref[size:] = tail.astype(jnp.int16)


def decode_sum_kernel(code_ref, out_ref):
    size = out_ref.shape[0]
    total = None
    for part in range(code_ref.shape[0]):
        tail = code_ref[part, size:].astype(jnp.int32)
        value = code_ref[part, :size].astype(jnp.int32).astype(jnp.float32) * step_of(tail[0:1], tail[1:2])
        total = value if total is None else total + value
    out_ref[...] = total.astype(out_ref.dtype)


def decode_sum(codes):
    size = codes.shape[2]
    vmem = pl.BlockSpec(memory_space=pltpu.VMEM)
    return pl.pallas_call(
        decode_sum_kernel,
        out_shape=jax.ShapeDtypeStruct((size, size), jnp.bfloat16),
        in_specs=[vmem],
        out_specs=vmem,
    )(codes)


def gram_blocks(positions, tiles, items, size, done=None):
    offsets = sorted(items)
    ready = [] if done is None else [done]

    def kernel(positions_ref, *refs):
        halves = {offset: refs[2 * n : 2 * n + 2] for n, offset in enumerate(offsets)}
        out_ref = refs[-1]
        for tile in tiles:
            for chip in range(out_ref.shape[1]):
                position = positions_ref[tile, chip]
                left_row = pl.ds(pl.multiple_of(lax.shift_right_logical(position, 2) * size, size), size)
                right_row = pl.ds(pl.multiple_of(lax.bitwise_and(position, 3) * size, size), size)
                left, right = TILES[tile]
                total = None
                for left_ref, right_ref in zip(halves[left], halves[right]):
                    product = lax.dot_general(
                        left_ref[left_row, :],
                        right_ref[right_row, :],
                        (((1,), (1,)), ((), ())),
                        preferred_element_type=jnp.float32,
                    )
                    total = product if total is None else total + product
                encode(total, out_ref.at[tile - tiles[0], chip])
        if ready:
            out_ref[len(tiles) :] = refs[-2][...]

    count = len(tiles) + (done.shape[0] if ready else 0)
    vmem = pl.BlockSpec(memory_space=pltpu.VMEM)
    operands = [half for offset in offsets for half in items[offset]] + ready
    return pl.pallas_call(
        kernel,
        out_shape=jax.ShapeDtypeStruct((count, positions.shape[1], size + TAIL, size), jnp.int16),
        in_specs=[pl.BlockSpec(memory_space=pltpu.SMEM)] + [vmem] * len(operands),
        out_specs=vmem,
        compiler_params=pltpu.CompilerParams(vmem_limit_bytes=48 * 2**20),
    )(positions, *operands)


def moved(value, axis, target):
    count = lax.axis_size(axis)
    return lax.ppermute(value, axis, [(source, target(source)) for source in range(count)])


def on_device(x_vals, x_rows, out_block):
    row_count = lax.axis_size("row")
    col_count = lax.axis_size("col")
    chip_count = lax.axis_size("chip")

    def up(value):
        return moved(value, "row", lambda r: (r + 1) % row_count)

    def down(value):
        return moved(value, "row", lambda r: (r - 1) % row_count)

    def swap_core(value):
        return moved(value, "core", lambda c: c ^ 1)

    def to_home(place):
        row, col = divmod(place, col_count)
        return (row + TILES[col][0]) % row_count * col_count + col

    own = densify(x_vals[0], x_rows[0], out_block.reshape(1))
    below = up(own)
    above = down(own)
    below2 = up(below)
    above2 = down(above)
    late_own, near = lax.optimization_barrier((own, jnp.stack([below, above])))
    near_other = swap_core(near)
    own_other = swap_core(late_own)
    above2_other = swap_core(above2)
    col = lax.axis_index("col")
    wanted = own[-1, :128]
    for shift, item in ((2, above2), (1, above), (-1, below)):
        for tile, (left, _) in enumerate(TILES):
            if left == shift:
                wanted = jnp.where(col == tile, item[-1, :128], wanted)
    spread = jnp.broadcast_to(wanted.astype(jnp.float32), (col_count * chip_count, 128))
    gathered_positions = lax.all_to_all(spread, ("col", "chip"), 0, 0, tiled=True)
    positions = gathered_positions[:, 0].astype(jnp.int32).reshape(col_count, chip_count)
    size = x_vals.shape[3]
    near_items = {
        0: (own, own_other),
        -1: (below, near_other[0]),
        1: (above, near_other[1]),
        2: (above2, above2_other),
    }
    partial_sums = gram_blocks(positions, NEAR, near_items, size)
    far_items = {
        0: (own, own_other),
        1: (above, near_other[1]),
        -2: (below2, swap_core(below2)),
        2: (above2, above2_other),
    }
    partial_sums = gram_blocks(positions, FAR, far_items, size, partial_sums)
    partial_sums = partial_sums.reshape((-1,) + partial_sums.shape[2:])
    gathered = lax.all_to_all(partial_sums, ("col", "chip"), 0, 0, tiled=True)
    total = decode_sum(gathered)
    result = moved(total, ("row", "col"), to_home)
    return result.reshape(out_block.shape + x_vals.shape[3:])


def solution(mesh):
    shape = dict(mesh.shape)
    devices = mesh.devices.reshape(shape["row"], shape["col"], shape["depth"] // 2, 2)
    fine_mesh = jax.sharding.Mesh(devices, ("row", "col", "chip", "core"))
    depth = ("chip", "core")
    in_specs = (
        P("row", ("col",) + depth, None, None, None),
        P("row", ("col",) + depth, None),
        P("row", "col", depth),
    )
    out_specs = P("row", "col", depth, None, None)
    return jax.shard_map(
        on_device, mesh=fine_mesh, in_specs=in_specs, out_specs=out_specs, check_vma=False
    )
```

```python
import jax
import jax.numpy as jnp
from jax import lax
from jax.experimental import pallas as pl
from jax.experimental.pallas import tpu as pltpu
from jax.sharding import PartitionSpec as P

TILES = ((2, -2), (1, -2), (0, -2), (0, -1), (0, 0), (0, 1), (0, 2), (-1, 2))

NEAR = (3, 4, 5, 6, 7)
FAR = (0, 1, 2)
LEVELS = 32766.0
TAIL = 8
NOTE = 16


def dense_kernel(rows_ref, wanted_ref, vals_ref, out_ref):
    columns, slots, size, width = vals_ref.shape
    for column in range(columns):
        for row in range(slots):
            slot = jnp.int32(-1)
            for candidate in range(slots):
                slot = jnp.where(rows_ref[column, candidate] == row, candidate, slot)
            at = (slice(row * size, (row + 1) * size), slice(column * width, (column + 1) * width))

            @pl.when(slot >= 0)
            def _():
                out_ref[at] = vals_ref[column, slot]

            @pl.when(slot < 0)
            def _():
                out_ref[at] = jnp.zeros((size, width), out_ref.dtype)

    note = jnp.full((NOTE, columns * width), wanted_ref[0], jnp.int32)
    out_ref[slots * size :] = note.astype(jnp.float32).astype(out_ref.dtype)


def densify(x_vals, x_rows, wanted):
    columns, slots, size, width = x_vals.shape
    smem = pl.BlockSpec(memory_space=pltpu.SMEM)
    vmem = pl.BlockSpec(memory_space=pltpu.VMEM)
    return pl.pallas_call(
        dense_kernel,
        out_shape=jax.ShapeDtypeStruct((slots * size + NOTE, columns * width), x_vals.dtype),
        in_specs=[smem, smem, vmem],
        out_specs=vmem,
    )(x_rows, wanted, x_vals)


def step_of(exponent, mantissa):
    return mantissa.astype(jnp.float32) * jnp.exp2((exponent - 14).astype(jnp.float32)) * (1.0 / LEVELS)


def encode(value, code_ref):
    size = value.shape[0]
    peak = jnp.maximum(jnp.max(jnp.abs(value), axis=0, keepdims=True), 1e-30)
    exponent = jnp.ceil(jnp.log2(peak))
    mantissa = jnp.ceil(peak * jnp.exp2(14.0 - exponent)) + 1.0
    exponent = exponent.astype(jnp.int32)
    mantissa = mantissa.astype(jnp.int32)
    code = jnp.floor(value * (1.0 / step_of(exponent, mantissa)) + 0.5)
    code_ref[:size] = code.astype(jnp.int32).astype(jnp.int16)
    line = lax.broadcasted_iota(jnp.int32, (TAIL, value.shape[1]), 0)
    tail = jnp.where(line == 0, exponent, jnp.where(line == 1, mantissa, 0))
    code_ref[size:] = tail.astype(jnp.int16)


def decode_sum(codes):
    size = codes.shape[2]
    steps = codes[:, size : size + 2].astype(jnp.int32)
    steps = step_of(steps[:, :1], steps[:, 1:])
    return jnp.sum(codes[:, :size].astype(jnp.float32) * steps, axis=0).astype(jnp.bfloat16)


def gram_blocks(positions, tiles, items, size, done=None):
    offsets = sorted(items)
    ready = [] if done is None else [done]

    def kernel(positions_ref, *refs):
        halves = {offset: refs[2 * n : 2 * n + 2] for n, offset in enumerate(offsets)}
        out_ref = refs[-1]
        for tile in tiles:
            for chip in range(out_ref.shape[1]):
                position = positions_ref[tile, chip]
                left_row = pl.ds(pl.multiple_of(lax.shift_right_logical(position, 2) * size, size), size)
                right_row = pl.ds(pl.multiple_of(lax.bitwise_and(position, 3) * size, size), size)
                left, right = TILES[tile]
                total = None
                for left_ref, right_ref in zip(halves[left], halves[right]):
                    product = lax.dot_general(
                        left_ref[left_row, :],
                        right_ref[right_row, :],
                        (((1,), (1,)), ((), ())),
                        preferred_element_type=jnp.float32,
                    )
                    total = product if total is None else total + product
                encode(total, out_ref.at[tile - tiles[0], chip])
        if ready:
            out_ref[len(tiles) :] = refs[-2][...]

    count = len(tiles) + (done.shape[0] if ready else 0)
    vmem = pl.BlockSpec(memory_space=pltpu.VMEM)
    operands = [half for offset in offsets for half in items[offset]] + ready
    return pl.pallas_call(
        kernel,
        out_shape=jax.ShapeDtypeStruct((count, positions.shape[1], size + TAIL, size), jnp.int16),
        in_specs=[pl.BlockSpec(memory_space=pltpu.SMEM)] + [vmem] * len(operands),
        out_specs=vmem,
        compiler_params=pltpu.CompilerParams(vmem_limit_bytes=48 * 2**20),
    )(positions, *operands)


def moved(value, axis, target):
    count = lax.axis_size(axis)
    return lax.ppermute(value, axis, [(source, target(source)) for source in range(count)])


def on_device(x_vals, x_rows, out_block):
    row_count = lax.axis_size("row")
    col_count = lax.axis_size("col")
    chip_count = lax.axis_size("chip")

    def up(value):
        return moved(value, "row", lambda r: (r + 1) % row_count)

    def down(value):
        return moved(value, "row", lambda r: (r - 1) % row_count)

    def swap_core(value):
        return moved(value, "core", lambda c: c ^ 1)

    def to_home(place):
        row, col = divmod(place, col_count)
        return (row + TILES[col][0]) % row_count * col_count + col

    own = densify(x_vals[0], x_rows[0], out_block.reshape(1))
    below = up(own)
    above = down(own)
    below2 = up(below)
    above2 = down(above)
    late_own, near = lax.optimization_barrier((own, jnp.stack([below, above])))
    near_other = swap_core(near)
    own_other = swap_core(late_own)
    above2_other = swap_core(above2)
    col = lax.axis_index("col")
    wanted = own[-1, :128]
    for shift, item in ((2, above2), (1, above), (-1, below)):
        for tile, (left, _) in enumerate(TILES):
            if left == shift:
                wanted = jnp.where(col == tile, item[-1, :128], wanted)
    spread = jnp.broadcast_to(wanted.astype(jnp.float32), (col_count * chip_count, 128))
    gathered_positions = lax.all_to_all(spread, ("col", "chip"), 0, 0, tiled=True)
    positions = gathered_positions[:, 0].astype(jnp.int32).reshape(col_count, chip_count)
    size = x_vals.shape[3]
    near_items = {
        0: (own, own_other),
        -1: (below, near_other[0]),
        1: (above, near_other[1]),
        2: (above2, above2_other),
    }
    partial_sums = gram_blocks(positions, NEAR, near_items, size)
    far_items = {
        0: (own, own_other),
        1: (above, near_other[1]),
        -2: (below2, swap_core(below2)),
        2: (above2, above2_other),
    }
    partial_sums = gram_blocks(positions, FAR, far_items, size, partial_sums)
    partial_sums = partial_sums.reshape((-1,) + partial_sums.shape[2:])
    gathered = lax.all_to_all(partial_sums, ("col", "chip"), 0, 0, tiled=True)
    total = decode_sum(gathered)
    result = moved(total, ("row", "col"), to_home)
    return result.reshape(out_block.shape + x_vals.shape[3:])


def solution(mesh):
    shape = dict(mesh.shape)
    devices = mesh.devices.reshape(shape["row"], shape["col"], shape["depth"] // 2, 2)
    fine_mesh = jax.sharding.Mesh(devices, ("row", "col", "chip", "core"))
    depth = ("chip", "core")
    in_specs = (
        P("row", ("col",) + depth, None, None, None),
        P("row", ("col",) + depth, None),
        P("row", "col", depth),
    )
    out_specs = P("row", "col", depth, None, None)
    return jax.shard_map(
        on_device, mesh=fine_mesh, in_specs=in_specs, out_specs=out_specs, check_vma=False
    )
```

```python
import jax
import jax.numpy as jnp
from jax import lax
from jax.experimental import pallas as pl
from jax.experimental.pallas import tpu as pltpu
from jax.sharding import PartitionSpec as P

TILES = ((2, -2), (1, -2), (0, -2), (0, -1), (0, 0), (0, 1), (0, 2), (-1, 2))

NEAR = (3, 4, 5, 6, 7)
FAR = (0, 1, 2)
LEVELS = 32766.0
TAIL = 8
NOTE = 16


def dense_kernel(rows_ref, wanted_ref, vals_ref, out_ref):
    columns, slots, size, width = vals_ref.shape
    for column in range(columns):
        for row in range(slots):
            slot = jnp.int32(-1)
            for candidate in range(slots):
                slot = jnp.where(rows_ref[column, candidate] == row, candidate, slot)
            at = (slice(row * size, (row + 1) * size), slice(column * width, (column + 1) * width))

            @pl.when(slot >= 0)
            def _():
                out_ref[at] = vals_ref[column, slot]

            @pl.when(slot < 0)
            def _():
                out_ref[at] = jnp.zeros((size, width), out_ref.dtype)

    note = jnp.full((NOTE, columns * width), wanted_ref[0], jnp.int32)
    out_ref[slots * size :] = note.astype(jnp.float32).astype(out_ref.dtype)


def densify(x_vals, x_rows, wanted):
    columns, slots, size, width = x_vals.shape
    smem = pl.BlockSpec(memory_space=pltpu.SMEM)
    vmem = pl.BlockSpec(memory_space=pltpu.VMEM)
    return pl.pallas_call(
        dense_kernel,
        out_shape=jax.ShapeDtypeStruct((slots * size + NOTE, columns * width), x_vals.dtype),
        in_specs=[smem, smem, vmem],
        out_specs=vmem,
    )(x_rows, wanted, x_vals)


def step_of(exponent, mantissa):
    return mantissa.astype(jnp.float32) * jnp.exp2((exponent - 14).astype(jnp.float32)) * (1.0 / LEVELS)


def encode(value, code_ref):
    size = value.shape[0]
    peak = jnp.maximum(jnp.max(jnp.abs(value), axis=0, keepdims=True), 1e-30)
    exponent = jnp.ceil(jnp.log2(peak))
    mantissa = jnp.ceil(peak * jnp.exp2(14.0 - exponent)) + 1.0
    exponent = exponent.astype(jnp.int32)
    mantissa = mantissa.astype(jnp.int32)
    code = jnp.floor(value * (1.0 / step_of(exponent, mantissa)) + 0.5)
    code_ref[:size] = code.astype(jnp.int32).astype(jnp.int16)
    line = lax.broadcasted_iota(jnp.int32, (TAIL, value.shape[1]), 0)
    tail = jnp.where(line == 0, exponent, jnp.where(line == 1, mantissa, 0))
    code_ref[size:] = tail.astype(jnp.int16)


def decode_sum(codes):
    size = codes.shape[2]
    steps = codes[:, size : size + 2].astype(jnp.int32)
    steps = step_of(steps[:, :1], steps[:, 1:])
    return jnp.sum(codes[:, :size].astype(jnp.float32) * steps, axis=0).astype(jnp.bfloat16)


def gram_blocks(positions, tiles, items, size, done=None):
    offsets = sorted(items)
    ready = [] if done is None else [done]

    def kernel(positions_ref, *refs):
        halves = {offset: refs[2 * n : 2 * n + 2] for n, offset in enumerate(offsets)}
        out_ref = refs[-1]
        for tile in tiles:
            for chip in range(out_ref.shape[1]):
                position = positions_ref[tile, chip]
                left_row = pl.ds(pl.multiple_of(lax.shift_right_logical(position, 2) * size, size), size)
                right_row = pl.ds(pl.multiple_of(lax.bitwise_and(position, 3) * size, size), size)
                left, right = TILES[tile]
                total = None
                for left_ref, right_ref in zip(halves[left], halves[right]):
                    product = lax.dot_general(
                        left_ref[left_row, :],
                        right_ref[right_row, :],
                        (((1,), (1,)), ((), ())),
                        preferred_element_type=jnp.float32,
                    )
                    total = product if total is None else total + product
                encode(total, out_ref.at[tile - tiles[0], chip])
        if ready:
            out_ref[len(tiles) :] = refs[-2][...]

    count = len(tiles) + (done.shape[0] if ready else 0)
    vmem = pl.BlockSpec(memory_space=pltpu.VMEM)
    operands = [half for offset in offsets for half in items[offset]] + ready
    return pl.pallas_call(
        kernel,
        out_shape=jax.ShapeDtypeStruct((count, positions.shape[1], size + TAIL, size), jnp.int16),
        in_specs=[pl.BlockSpec(memory_space=pltpu.SMEM)] + [vmem] * len(operands),
        out_specs=vmem,
        compiler_params=pltpu.CompilerParams(vmem_limit_bytes=48 * 2**20),
    )(positions, *operands)


def moved(value, axis, target):
    count = lax.axis_size(axis)
    return lax.ppermute(value, axis, [(source, target(source)) for source in range(count)])


def on_device(x_vals, x_rows, out_block):
    row_count = lax.axis_size("row")
    col_count = lax.axis_size("col")
    chip_count = lax.axis_size("chip")

    def up(value):
        return moved(value, "row", lambda r: (r + 1) % row_count)

    def down(value):
        return moved(value, "row", lambda r: (r - 1) % row_count)

    def swap_core(value):
        return moved(value, "core", lambda c: c ^ 1)

    def to_home(place):
        row, col = divmod(place, col_count)
        return (row + TILES[col][0]) % row_count * col_count + col

    own = densify(x_vals[0], x_rows[0], out_block.reshape(1))
    below = up(own)
    above = down(own)
    below2 = up(below)
    above2 = down(above)
    near_other = swap_core(jnp.stack([below, above]))
    own_other, above2_other = swap_core(jnp.stack([own, above2]))
    col = lax.axis_index("col")
    wanted = own[-1, :128]
    for shift, item in ((2, above2), (1, above), (-1, below)):
        for tile, (left, _) in enumerate(TILES):
            if left == shift:
                wanted = jnp.where(col == tile, item[-1, :128], wanted)
    spread = jnp.broadcast_to(wanted.astype(jnp.float32), (col_count * chip_count, 128))
    gathered_positions = lax.all_to_all(spread, ("col", "chip"), 0, 0, tiled=True)
    positions = gathered_positions[:, 0].astype(jnp.int32).reshape(col_count, chip_count)
    size = x_vals.shape[3]
    near_items = {
        0: (own, own_other),
        -1: (below, near_other[0]),
        1: (above, near_other[1]),
        2: (above2, above2_other),
    }
    partial_sums = gram_blocks(positions, NEAR, near_items, size)
    far_items = {
        0: (own, own_other),
        1: (above, near_other[1]),
        -2: (below2, swap_core(below2)),
        2: (above2, above2_other),
    }
    partial_sums = gram_blocks(positions, FAR, far_items, size, partial_sums)
    partial_sums = partial_sums.reshape((-1,) + partial_sums.shape[2:])
    gathered = lax.all_to_all(partial_sums, ("col", "chip"), 0, 0, tiled=True)
    total = decode_sum(gathered)
    result = moved(total, ("row", "col"), to_home)
    return result.reshape(out_block.shape + x_vals.shape[3:])


def solution(mesh):
    shape = dict(mesh.shape)
    devices = mesh.devices.reshape(shape["row"], shape["col"], shape["depth"] // 2, 2)
    fine_mesh = jax.sharding.Mesh(devices, ("row", "col", "chip", "core"))
    depth = ("chip", "core")
    in_specs = (
        P("row", ("col",) + depth, None, None, None),
        P("row", ("col",) + depth, None),
        P("row", "col", depth),
    )
    out_specs = P("row", "col", depth, None, None)
    return jax.shard_map(
        on_device, mesh=fine_mesh, in_specs=in_specs, out_specs=out_specs, check_vma=False
    )
```

```python
import jax
import jax.numpy as jnp
from jax import lax
from jax.experimental import pallas as pl
from jax.experimental.pallas import tpu as pltpu
from jax.sharding import PartitionSpec as P

TILES = ((2, -2), (1, -2), (0, -2), (0, -1), (0, 0), (0, 1), (0, 2), (-1, 2))

NEAR = (3, 4, 5, 6, 7)
FAR = (0, 1, 2)
LEVELS = 32766.0
TAIL = 8
NOTE = 16


def dense_kernel(rows_ref, wanted_ref, vals_ref, out_ref):
    columns, slots, size, width = vals_ref.shape
    for column in range(columns):
        for row in range(slots):
            slot = jnp.int32(-1)
            for candidate in range(slots):
                slot = jnp.where(rows_ref[column, candidate] == row, candidate, slot)
            at = (slice(row * size, (row + 1) * size), slice(column * width, (column + 1) * width))

            @pl.when(slot >= 0)
            def _():
                out_ref[at] = vals_ref[column, slot]

            @pl.when(slot < 0)
            def _():
                out_ref[at] = jnp.zeros((size, width), out_ref.dtype)

    note = jnp.full((NOTE, columns * width), wanted_ref[0], jnp.int32)
    out_ref[slots * size :] = note.astype(jnp.float32).astype(out_ref.dtype)


def densify(x_vals, x_rows, wanted):
    columns, slots, size, width = x_vals.shape
    smem = pl.BlockSpec(memory_space=pltpu.SMEM)
    vmem = pl.BlockSpec(memory_space=pltpu.VMEM)
    return pl.pallas_call(
        dense_kernel,
        out_shape=jax.ShapeDtypeStruct((slots * size + NOTE, columns * width), x_vals.dtype),
        in_specs=[smem, smem, vmem],
        out_specs=vmem,
    )(x_rows, wanted, x_vals)


def step_of(exponent, mantissa):
    return mantissa.astype(jnp.float32) * jnp.exp2((exponent - 14).astype(jnp.float32)) * (1.0 / LEVELS)


def encode(value, code_ref):
    size = value.shape[0]
    peak = jnp.maximum(jnp.max(jnp.abs(value), axis=0, keepdims=True), 1e-30)
    exponent = jnp.ceil(jnp.log2(peak))
    mantissa = jnp.ceil(peak * jnp.exp2(14.0 - exponent)) + 1.0
    exponent = exponent.astype(jnp.int32)
    mantissa = mantissa.astype(jnp.int32)
    code = jnp.floor(value * (1.0 / step_of(exponent, mantissa)) + 0.5)
    code_ref[:size] = code.astype(jnp.int32).astype(jnp.int16)
    line = lax.broadcasted_iota(jnp.int32, (TAIL, value.shape[1]), 0)
    tail = jnp.where(line == 0, exponent, jnp.where(line == 1, mantissa, 0))
    code_ref[size:] = tail.astype(jnp.int16)


def decode_sum(codes):
    size = codes.shape[2]
    steps = codes[:, size : size + 2].astype(jnp.int32)
    steps = step_of(steps[:, :1], steps[:, 1:])
    return jnp.sum(codes[:, :size].astype(jnp.float32) * steps, axis=0).astype(jnp.bfloat16)


def gram_blocks(positions, tiles, items, size, done=None):
    offsets = sorted(items)
    ready = [] if done is None else [done]

    def kernel(positions_ref, *refs):
        halves = {offset: refs[2 * n : 2 * n + 2] for n, offset in enumerate(offsets)}
        out_ref = refs[-1]
        for tile in tiles:
            for chip in range(out_ref.shape[1]):
                position = positions_ref[tile, chip]
                left_row = pl.ds(pl.multiple_of(lax.shift_right_logical(position, 2) * size, size), size)
                right_row = pl.ds(pl.multiple_of(lax.bitwise_and(position, 3) * size, size), size)
                left, right = TILES[tile]
                total = None
                for left_ref, right_ref in zip(halves[left], halves[right]):
                    product = lax.dot_general(
                        left_ref[left_row, :],
                        right_ref[right_row, :],
                        (((1,), (1,)), ((), ())),
                        preferred_element_type=jnp.float32,
                    )
                    total = product if total is None else total + product
                encode(total, out_ref.at[tile - tiles[0], chip])
        if ready:
            out_ref[len(tiles) :] = refs[-2][...]

    count = len(tiles) + (done.shape[0] if ready else 0)
    vmem = pl.BlockSpec(memory_space=pltpu.VMEM)
    operands = [half for offset in offsets for half in items[offset]] + ready
    return pl.pallas_call(
        kernel,
        out_shape=jax.ShapeDtypeStruct((count, positions.shape[1], size + TAIL, size), jnp.int16),
        in_specs=[pl.BlockSpec(memory_space=pltpu.SMEM)] + [vmem] * len(operands),
        out_specs=vmem,
        compiler_params=pltpu.CompilerParams(vmem_limit_bytes=48 * 2**20),
    )(positions, *operands)


def moved(value, axis, target):
    count = lax.axis_size(axis)
    return lax.ppermute(value, axis, [(source, target(source)) for source in range(count)])


def on_device(x_vals, x_rows, out_block):
    row_count = lax.axis_size("row")
    col_count = lax.axis_size("col")
    chip_count = lax.axis_size("chip")

    def up(value):
        return moved(value, "row", lambda r: (r + 1) % row_count)

    def down(value):
        return moved(value, "row", lambda r: (r - 1) % row_count)

    def swap_core(value):
        return moved(value, "core", lambda c: c ^ 1)

    def to_home(place):
        row, col = divmod(place, col_count)
        return (row + TILES[col][0]) % row_count * col_count + col

    own = densify(x_vals[0], x_rows[0], out_block.reshape(1))
    below = up(own)
    above = down(own)
    below2 = up(below)
    above2 = down(above)
    own_other, above_other = swap_core(jnp.stack([own, above]))
    below_other, above2_other = swap_core(jnp.stack([below, above2]))
    col = lax.axis_index("col")
    wanted = own[-1, :128]
    for shift, item in ((2, above2), (1, above), (-1, below)):
        for tile, (left, _) in enumerate(TILES):
            if left == shift:
                wanted = jnp.where(col == tile, item[-1, :128], wanted)
    spread = jnp.broadcast_to(wanted.astype(jnp.float32), (col_count * chip_count, 128))
    gathered_positions = lax.all_to_all(spread, ("col", "chip"), 0, 0, tiled=True)
    positions = gathered_positions[:, 0].astype(jnp.int32).reshape(col_count, chip_count)
    size = x_vals.shape[3]
    near_items = {
        0: (own, own_other),
        -1: (below, below_other),
        1: (above, above_other),
        2: (above2, above2_other),
    }
    partial_sums = gram_blocks(positions, NEAR, near_items, size)
    far_items = {
        0: (own, own_other),
        1: (above, above_other),
        -2: (below2, swap_core(below2)),
        2: (above2, above2_other),
    }
    partial_sums = gram_blocks(positions, FAR, far_items, size, partial_sums)
    partial_sums = partial_sums.reshape((-1,) + partial_sums.shape[2:])
    gathered = lax.all_to_all(partial_sums, ("col", "chip"), 0, 0, tiled=True)
    total = decode_sum(gathered)
    result = moved(total, ("row", "col"), to_home)
    return result.reshape(out_block.shape + x_vals.shape[3:])


def solution(mesh):
    shape = dict(mesh.shape)
    devices = mesh.devices.reshape(shape["row"], shape["col"], shape["depth"] // 2, 2)
    fine_mesh = jax.sharding.Mesh(devices, ("row", "col", "chip", "core"))
    depth = ("chip", "core")
    in_specs = (
        P("row", ("col",) + depth, None, None, None),
        P("row", ("col",) + depth, None),
        P("row", "col", depth),
    )
    out_specs = P("row", "col", depth, None, None)
    return jax.shard_map(
        on_device, mesh=fine_mesh, in_specs=in_specs, out_specs=out_specs, check_vma=False
    )
```
